32 devices in a mesh: groups: 2 (over x), ta: 4 (over y, core), xy: 4 (over z).
Axes of the slice: x: 2, y: 2, z: 4, core: 2. Of those that a mesh axis runs over, the one named last changes fastest.
Arguments:
- sources: bfloat16 [8, 4, 4, 8, 96, 256], P('groups', 'ta', 'xy'), parts along dimension 0, may hold values from -24 to 24
- coarse_links: bfloat16 [18, 4, 4, 4, 8, 96, 96], P('groups', None, 'ta', 'xy'), parts along dimension 0, may hold values from -0.119628906 to 0.119628906
Outputs:
- solution: float32 [8, 4, 4, 8, 96, 256], P('groups', 'ta', 'xy'), parts along dimension 0
The draws below stay inside these ranges and needn't reach their ends.
There are 2 independent parts, one for each index of `groups`. The reference program is written for one: setup_inputs(seed, part) draws one part's arguments, and reference() takes and returns one part's arrays. A program takes and returns all parts, laid end to end along the dimension named above; each array names one. Nothing has to cross between parts.
All inputs are finite; a program needn't handle non-finite values.
Results may differ from the reference program's by a relative error of at most 0.0019.
The reference program's roundings to bfloat16 on the way count: a program that leaves them out, or rounds other values in their place, can miss the bound.
Values may be sent and summed in bfloat16 or wider, within the bound.
A program may use at most 128 MiB of HBM per device.

```python
import jax
import jax.numpy as jnp
from jax import lax

COMP = 96
RHS = 256
NY = 4
NZ = 8
DIRS = 9
ITERS = 2
NT = 4
NX = 4


def draw_sources(key, part):
    full_shape = (NY, NT, NX, NZ, COMP, RHS)
    subkeys = jax.random.split(jax.random.fold_in(key, 17), 4)
    rising = 1.5 * 3.0 ** (jnp.arange(NT, dtype=jnp.float32) / max(NT - 1, 1))
    rising = rising.reshape(1, NT, 1, 1, 1, 1)
    values = jax.random.normal(subkeys[3], full_shape, jnp.float32) * rising
    return jnp.clip(values, -24.0, 24.0).astype(jnp.bfloat16)


def shard_levels(rng, dims, cuts, smallest, high):
    def one(dim, blocks):
        heights = jax.random.uniform(jax.random.fold_in(jax.random.fold_in(rng, 6), dim), (blocks,), jnp.float32, smallest / len(cuts), high / len(cuts))
        return jnp.repeat(jnp.exp(heights), dims[dim] // blocks).reshape((-1,) + (1,) * (len(dims) - dim - 1))

    loudness = one(*cuts[0])
    for cut in cuts[1:]:
        loudness = loudness * one(*cut)
    return loudness


def noise(key, shape, width, bound, shards=(), kind=jnp.bfloat16):
    gain = shard_levels(key, shape, shards, -0.22, 0.18) if shards else 1.0
    array = jax.random.normal(key, shape, jnp.float32) * width * gain
    return jnp.minimum(jnp.maximum(array, -bound), bound).astype(kind)


def setup_inputs(seed: int = 0, part: int = 0) -> dict:
    splits = jax.random.split(jax.random.key(seed), 3)
    own_keys = jax.random.split(jax.random.fold_in(splits[2], part), 3)
    return {
        "sources": draw_sources(jax.random.fold_in(jax.random.fold_in(splits[2], part), 71), part),
        "coarse_links": noise(own_keys[1], (DIRS, NY, NT, NX, NZ, COMP, COMP), 0.02, 0.119628906, ((2, 4), (3, 4))),
    }


mass_term = 2.0
direction_moves = ((1, 1), (1, -1), (2, 1), (2, -1), (0, 1), (0, -1), (3, 1), (3, -1))

def link_product(link_field, vector, flipped):
    einsum_form = 'abcio,abcir->abcor' if flipped else 'abcoi,abcir->abcor'

    def one_plane(plane_pair):
        link_plane, values = plane_pair
        matrix = link_plane.astype(jnp.float32)
        entries = values.astype(jnp.float32)
        return jnp.einsum(einsum_form, matrix, entries, precision=lax.Precision.HIGHEST)
    return lax.map(one_plane, (link_field, vector))

def apply_forward(rounded, coarse_links):
    summed = mass_term * rounded.astype(jnp.float32) + link_product(coarse_links[0], rounded, False)
    for number in range(8):
        axis_number, sign_value = direction_moves[number]
        summed = summed + link_product(coarse_links[number + 1], jnp.roll(rounded, -sign_value, axis_number), False)
    return summed

def apply_adjoint(image_vec, coarse_links):
    summed = mass_term * image_vec.astype(jnp.float32) + link_product(coarse_links[0], image_vec, True)
    for number in range(8):
        axis_number, sign_value = direction_moves[number]
        adjoint_term = link_product(coarse_links[number + 1], image_vec, True).astype(jnp.bfloat16)
        summed = summed + jnp.roll(adjoint_term, sign_value, axis_number).astype(jnp.float32)
    return summed

def gram(left_vec, right_vec):
    left_rows = left_vec.reshape(-1, COMP, RHS)
    right_rows = right_vec.reshape(-1, COMP, RHS)
    return jnp.einsum('sir,sit->rt', left_rows, right_rows, precision=lax.Precision.HIGHEST)

def combine(vector, coefficients):
    return jnp.einsum('abcdir,rt->abcdit', vector, coefficients, precision=lax.Precision.HIGHEST)

def solve_spd(matrix, right_side):
    factor = jnp.linalg.cholesky(matrix)
    return jax.scipy.linalg.cho_solve((factor, True), right_side)

def reference(sources, coarse_links):
    residual = sources.astype(jnp.float32)
    solution = jnp.zeros_like(residual)
    search = residual
    energy = gram(residual, residual)
    for iteration in range(ITERS):
        rounded = search.astype(jnp.bfloat16)
        image_vec = apply_forward(rounded, coarse_links).astype(jnp.bfloat16)
        normal_image = apply_adjoint(image_vec, coarse_links)
        alpha_step = solve_spd(gram(search, normal_image), energy)
        solution = solution + combine(search, alpha_step)
        if iteration + 1 < ITERS:
            residual = residual - combine(normal_image, alpha_step)
            fresh_energy = gram(residual, residual)
            beta_step = solve_spd(energy, fresh_energy)
            search = residual + combine(search, beta_step)
            energy = fresh_energy
    return solution
```

```python
import functools

import jax
import jax.numpy as jnp
from jax import lax
from jax.experimental import pallas as pl
from jax.experimental.pallas import tpu as pltpu
from jax.sharding import PartitionSpec as P

ITERS = 2
mass_term = 2.0
MESH = pl.DeviceIdType.MESH
HI = lax.Precision.HIGHEST
f32 = jnp.float32
bf16 = jnp.bfloat16


def sum_kernel(n_ta, n_xy, x_ref, o_ref, parts, whole, send1, recv1, send2, recv2):
    n = n_ta * n_xy
    me = lax.axis_index("ta") * n_xy + lax.axis_index("xy")

    def device(off):
        peer = lax.rem(me + off, n)
        return peer, {"ta": peer // n_xy, "xy": lax.rem(peer, n_xy)}

    def first(off):
        peer, where = device(off)
        return pltpu.make_async_remote_copy(
            src_ref=x_ref.at[peer], dst_ref=parts.at[off], send_sem=send1.at[off],
            recv_sem=recv1.at[off], device_id=where, device_id_type=MESH)

    def second(off):
        _, where = device(off)
        return pltpu.make_async_remote_copy(
            src_ref=whole.at[me], dst_ref=whole.at[me], send_sem=send2.at[off],
            recv_sem=recv2.at[off], device_id=where, device_id_type=MESH)

    def arrived(off):
        peer = lax.rem(me + n - off, n)
        return pltpu.make_async_remote_copy(
            src_ref=whole.at[peer], dst_ref=whole.at[peer], send_sem=send2.at[off],
            recv_sem=recv2.at[off], device_id=device(off)[1], device_id_type=MESH)

    barrier = pltpu.get_barrier_semaphore()

    @pl.loop(1, n)
    def _(off):
        pl.semaphore_signal(barrier, inc=1, device_id=device(off)[1], device_id_type=MESH)

    pl.semaphore_wait(barrier, n - 1)

    @pl.loop(1, n)
    def _(off):
        first(off).start()

    @pl.loop(1, n)
    def _(off):
        first(off).wait_recv()

    acc = x_ref[me]
    for off in range(1, n):
        acc = acc + parts[off]
    whole[me] = acc

    @pl.loop(1, n)
    def _(off):
        second(off).start()

    @pl.loop(1, n)
    def _(off):
        arrived(off).wait_recv()

    o_ref[...] = whole[...]

    @pl.loop(1, n)
    def _(off):
        first(off).wait_send()
        second(off).wait_send()


def all_sum(matrix):
    n_ta, n_xy = lax.axis_size("ta"), lax.axis_size("xy")
    n = n_ta * n_xy
    rows, cols = matrix.shape
    per = -(-rows // n)
    padded = jnp.pad(matrix, ((0, per * n - rows), (0, 0))) if per * n != rows else matrix
    shape = (n, per, cols)
    out = pl.pallas_call(
        functools.partial(sum_kernel, n_ta, n_xy),
        out_shape=jax.ShapeDtypeStruct(shape, f32),
        in_specs=[pl.BlockSpec(memory_space=pltpu.VMEM)],
        out_specs=pl.BlockSpec(memory_space=pltpu.VMEM),
        scratch_shapes=[pltpu.VMEM(shape, f32), pltpu.VMEM(shape, f32)]
        + [pltpu.SemaphoreType.DMA((n,))] * 4,
        compiler_params=pltpu.CompilerParams(collective_id=0, has_side_effects=True),
    )(padded.reshape(shape))
    return out.reshape(n * per, cols)[:rows]


def inverse_kernel(a_ref, x_ref, s_ref):
    n = a_ref.shape[0]
    dot = functools.partial(jnp.dot, precision=HI, preferred_element_type=f32)
    row = lax.broadcasted_iota(jnp.int32, (n, n), 0)
    col = lax.broadcasted_iota(jnp.int32, (n, n), 1)
    eye = jnp.where(row == col, 1.0, 0.0).astype(f32)
    a = a_ref[...]
    a = 0.5 * (a + a.T)
    diag = a * eye
    down = lax.rsqrt(jnp.sum(diag, axis=1, keepdims=True))
    across = lax.rsqrt(jnp.sum(diag, axis=0, keepdims=True))
    a = a * down * across
    s_ref[...] = a
    power = eye - a
    x = eye + power
    for _ in range(3):
        power = dot(power, power)
        x = x + dot(x, power)
    x_ref[...] = x
    left = eye - dot(a, x)
    worst = jnp.max(jnp.abs(left))

    @pl.when(jnp.logical_not(worst < 1e-3))
    def _():
        x_ref[...] = s_ref[...]

        def eliminate(k, carry):
            m = x_ref[...]
            pivot_row = x_ref[pl.ds(k, 1), :]
            here = col == k
            pivot_col = jnp.sum(jnp.where(here, m, 0.0), axis=1, keepdims=True)
            hit = here[:1]
            inv = 1.0 / jnp.sum(jnp.where(hit, pivot_row, 0.0), axis=1, keepdims=True)
            scaled = jnp.where(hit, inv, pivot_row * inv)
            m = jnp.where(here, 0.0, m) - pivot_col * scaled
            x_ref[...] = jnp.where(row == k, scaled, m)
            return carry

        lax.fori_loop(0, n, eliminate, 0)

    x = x_ref[...]
    x = x + dot(x, eye - dot(s_ref[...], x))
    x_ref[...] = x * down * across


def spd_inverse(matrix):
    spec = pl.BlockSpec(memory_space=pltpu.VMEM)
    return pl.pallas_call(
        inverse_kernel,
        out_shape=jax.ShapeDtypeStruct(matrix.shape, f32),
        in_specs=[spec],
        out_specs=spec,
        scratch_shapes=[pltpu.VMEM(matrix.shape, f32)],
        cost_estimate=pl.CostEstimate(flops=int(1.5e9), bytes_accessed=1 << 20, transcendentals=0),
    )(matrix)


def mm(a, b):
    return jnp.dot(a, b, precision=HI)


def solve(matrix, inverse, right):
    out = mm(inverse, right)
    sym = 0.5 * (matrix + matrix.T)
    return out + mm(inverse, right - mm(sym, out))


def link_product(link_field, vector, flipped):
    einsum_form = "abcdio,abcdir->abcdor" if flipped else "abcdoi,abcdir->abcdor"
    return jnp.einsum(einsum_form, link_field, vector, preferred_element_type=f32)


def shifted(vector, axis, dim, step):
    count, size = lax.axis_size(axis), vector.shape[dim]
    if step > 0:
        edge = lax.slice_in_dim(vector, 0, 1, axis=dim)
        came = lax.ppermute(edge, axis, [((i + 1) % count, i) for i in range(count)])
        rest = [lax.slice_in_dim(vector, 1, size, axis=dim)] if size > 1 else []
        pieces = rest + [came]
    else:
        edge = lax.slice_in_dim(vector, size - 1, size, axis=dim)
        came = lax.ppermute(edge, axis, [(i, (i + 1) % count) for i in range(count)])
        rest = [lax.slice_in_dim(vector, 0, size - 1, axis=dim)] if size > 1 else []
        pieces = [came] + rest
    return jnp.concatenate(pieces, axis=dim) if len(pieces) > 1 else pieces[0]


HOPS = (("ta", 1, 1), ("ta", 1, -1), ("xy", 2, 1), ("xy", 2, -1))
LOCAL = ((0, 1), (0, -1), (3, 1), (3, -1))


def apply_forward(rounded, links):
    far = [shifted(rounded, *hop) for hop in HOPS]
    total = mass_term * rounded.astype(f32) + link_product(links[0], rounded, False)
    for number, (dim, step) in enumerate(LOCAL):
        total = total + link_product(links[number + 5], jnp.roll(rounded, -step, dim), False)
    for number in range(4):
        total = total + link_product(links[number + 1], far[number], False)
    return total


def apply_adjoint(image, links):
    sent = [link_product(links[number + 1], image, True).astype(bf16) for number in range(4)]
    far = [shifted(sent[number], axis, dim, -step) for number, (axis, dim, step) in enumerate(HOPS)]
    total = mass_term * image.astype(f32) + link_product(links[0], image, True)
    for number, (dim, step) in enumerate(LOCAL):
        term = link_product(links[number + 5], image, True).astype(bf16)
        total = total + jnp.roll(term, step, dim).astype(f32)
    return total, far


def rows_of(vector):
    return vector.reshape((-1,) + vector.shape[-2:])


def gram(left, right, precision=None):
    return jnp.einsum("sir,sit->rt", rows_of(left), rows_of(right), precision=precision,
                      preferred_element_type=f32)


def image_gram(full, image):
    low = (full - image.astype(f32)).astype(bf16)
    return gram(image, image) + gram(low, image)


def combine(vector, coefficients):
    return jnp.einsum("abcdir,rt->abcdit", vector, coefficients, precision=HI,
                      preferred_element_type=f32)


def body(sources, links):
    residual = sources.astype(f32)
    energy = all_sum(gram(sources, sources))
    energy_inv = spd_inverse(energy)
    search = residual
    solution = None
    for iteration in range(ITERS):
        rounded = search.astype(bf16)
        full = apply_forward(rounded, links)
        image = full.astype(bf16)
        last = iteration + 1 == ITERS
        if not last:
            partial, far = apply_adjoint(image, links)
        curvature = all_sum(image_gram(full, image))
        alpha = solve(curvature, spd_inverse(curvature), energy)
        step = combine(search, alpha)
        solution = step if solution is None else solution + step
        if not last:
            for term in far:
                partial = partial + term.astype(f32)
            residual = residual - combine(partial, alpha)
            fresh = all_sum(gram(residual, residual, HI))
            beta = solve(energy, energy_inv, fresh)
            search = residual + combine(search, beta)
            energy = fresh
    return solution


def solution(mesh):
    return jax.shard_map(
        body,
        mesh=mesh,
        in_specs=(
            P("groups", "ta", "xy", None, None, None),
            P("groups", None, "ta", "xy", None, None, None),
        ),
        out_specs=P("groups", "ta", "xy", None, None, None),
        check_vma=False,
    )
```

```python
import functools

import jax
import jax.numpy as jnp
from jax import lax
from jax.experimental import pallas as pl
from jax.experimental.pallas import tpu as pltpu
from jax.sharding import PartitionSpec as P


mass_term = 2.0
MESH = pl.DeviceIdType.MESH
HI = lax.Precision.HIGHEST
f32 = jnp.float32
bf16 = jnp.bfloat16


def sum_kernel(n_ta, n_xy, x_ref, o_ref, parts, whole, send1, recv1, send2, recv2):
    n = n_ta * n_xy
    me = lax.axis_index("ta") * n_xy + lax.axis_index("xy")

    def device(off):
        peer = lax.rem(me + off, n)
        return peer, {"ta": peer // n_xy, "xy": lax.rem(peer, n_xy)}

    def first(off):
        peer, where = device(off)
        return pltpu.make_async_remote_copy(
            src_ref=x_ref.at[peer], dst_ref=parts.at[off], send_sem=send1.at[off],
            recv_sem=recv1.at[off], device_id=where, device_id_type=MESH)

    def second(off):
        _, where = device(off)
        return pltpu.make_async_remote_copy(
            src_ref=whole.at[me], dst_ref=whole.at[me], send_sem=send2.at[off],
            recv_sem=recv2.at[off], device_id=where, device_id_type=MESH)

    def arrived(off):
        peer = lax.rem(me + n - off, n)
        return pltpu.make_async_remote_copy(
            src_ref=whole.at[peer], dst_ref=whole.at[peer], send_sem=send2.at[off],
            recv_sem=recv2.at[off], device_id=device(off)[1], device_id_type=MESH)

    barrier = pltpu.get_barrier_semaphore()

    @pl.loop(1, n)
    def _(off):
        pl.semaphore_signal(barrier, inc=1, device_id=device(off)[1], device_id_type=MESH)

    pl.semaphore_wait(barrier, n - 1)

    @pl.loop(1, n)
    def _(off):
        first(off).start()

    @pl.loop(1, n)
    def _(off):
        first(off).wait_recv()

    acc = x_ref[me]
    for off in range(1, n):
        acc = acc + parts[off]
    whole[me] = acc

    @pl.loop(1, n)
    def _(off):
        second(off).start()

    @pl.loop(1, n)
    def _(off):
        arrived(off).wait_recv()

    o_ref[...] = whole[...]

    @pl.loop(1, n)
    def _(off):
        first(off).wait_send()
        second(off).wait_send()


def all_sum(matrix, number=0):
    n_ta, n_xy = lax.axis_size("ta"), lax.axis_size("xy")
    n = n_ta * n_xy
    rows, cols = matrix.shape
    per = -(-rows // n)
    padded = jnp.pad(matrix, ((0, per * n - rows), (0, 0))) if per * n != rows else matrix
    shape = (n, per, cols)
    out = pl.pallas_call(
        functools.partial(sum_kernel, n_ta, n_xy),
        out_shape=jax.ShapeDtypeStruct(shape, f32),
        in_specs=[pl.BlockSpec(memory_space=pltpu.VMEM)],
        out_specs=pl.BlockSpec(memory_space=pltpu.VMEM),
        scratch_shapes=[pltpu.VMEM(shape, f32), pltpu.VMEM(shape, f32)]
        + [pltpu.SemaphoreType.DMA((n,))] * 4,
        cost_estimate=pl.CostEstimate(flops=0, bytes_accessed=64 << 20, transcendentals=0),
        compiler_params=pltpu.CompilerParams(collective_id=number, has_side_effects=True),
    )(padded.reshape(shape))
    return out.reshape(n * per, cols)[:rows]


dot = functools.partial(jnp.dot, precision=HI, preferred_element_type=f32)


def dot_t(a, b):
    return lax.dot_general(a, b, (((0,), (0,)), ((), ())), precision=HI, preferred_element_type=f32)


def symmetric(a):
    return 0.5 * (a + a.T)


def invert(a, x_ref, s_ref):
    n = a.shape[0]
    row = lax.broadcasted_iota(jnp.int32, (n, n), 0)
    col = lax.broadcasted_iota(jnp.int32, (n, n), 1)
    eye = jnp.where(row == col, 1.0, 0.0).astype(f32)
    diag = a * eye
    down = lax.rsqrt(jnp.sum(diag, axis=1, keepdims=True))
    across = lax.rsqrt(jnp.sum(diag, axis=0, keepdims=True))
    a = a * down * across
    s_ref[...] = a
    power = eye - a
    x = eye + power
    for _ in range(3):
        power = dot(power, power)
        x = x + dot(x, power)
    x_ref[...] = x
    worst = jnp.max(jnp.abs(eye - dot(a, x)))

    @pl.when(jnp.logical_not(worst < 1e-3))
    def _():
        x_ref[...] = s_ref[...]

        def eliminate(k, carry):
            m = x_ref[...]
            pivot_row = x_ref[pl.ds(k, 1), :]
            here = col == k
            pivot_col = jnp.sum(jnp.where(here, m, 0.0), axis=1, keepdims=True)
            hit = here[:1]
            inv = 1.0 / jnp.sum(jnp.where(hit, pivot_row, 0.0), axis=1, keepdims=True)
            scaled = jnp.where(hit, inv, pivot_row * inv)
            m = jnp.where(here, 0.0, m) - pivot_col * scaled
            x_ref[...] = jnp.where(row == k, scaled, m)
            return carry

        lax.fori_loop(0, n, eliminate, 0)

    x = x_ref[...]
    x = x + dot(x, eye - dot(s_ref[...], x))
    return x * down * across


def solved(a, inverse, right):
    out = dot(inverse, right)
    return out + dot(inverse, right - dot(a, out))


def energy_kernel(energy_ref, o_ref, x_ref, s_ref):
    o_ref[...] = invert(symmetric(energy_ref[...]), x_ref, s_ref)


def alpha_kernel(curvature_ref, energy_ref, o_ref, x_ref, s_ref):
    curvature = symmetric(curvature_ref[...])
    inverse = invert(curvature, x_ref, s_ref)
    o_ref[...] = solved(curvature, inverse, energy_ref[...])


def closing_kernel(energy_ref, inverse_ref, curvature_ref, alpha_ref, fresh_ref, square_ref,
                   gamma_ref, alpha2_ref, x_ref, s_ref):
    fresh = fresh_ref[...]
    beta = solved(symmetric(energy_ref[...]), inverse_ref[...], fresh)
    second = square_ref[...] - dot_t(beta, dot(symmetric(curvature_ref[...]), beta))
    second = symmetric(second)
    inverse = invert(second, x_ref, s_ref)
    alpha2 = solved(second, inverse, fresh)
    alpha2_ref[...] = alpha2
    gamma_ref[...] = alpha_ref[...] + dot(beta, alpha2)


def small(kernel, count, *args):
    spec = pl.BlockSpec(memory_space=pltpu.VMEM)
    shape = args[0].shape
    out = pl.pallas_call(
        kernel,
        out_shape=[jax.ShapeDtypeStruct(shape, f32)] * count,
        in_specs=[spec] * len(args),
        out_specs=[spec] * count,
        scratch_shapes=[pltpu.VMEM(shape, f32)] * 2,
        cost_estimate=pl.CostEstimate(flops=int(4e9), bytes_accessed=1 << 20, transcendentals=0),
    )(*args)
    return out if count > 1 else out[0]


def link_product(link_field, vector, flipped):
    einsum_form = "abcdio,abcdir->abcdor" if flipped else "abcdoi,abcdir->abcdor"
    return jnp.einsum(einsum_form, link_field, vector, preferred_element_type=f32)


def shifted(vector, axis, dim, step):
    count, size = lax.axis_size(axis), vector.shape[dim]
    if step > 0:
        edge = lax.slice_in_dim(vector, 0, 1, axis=dim)
        came = lax.ppermute(edge, axis, [((i + 1) % count, i) for i in range(count)])
        rest = [lax.slice_in_dim(vector, 1, size, axis=dim)] if size > 1 else []
        pieces = rest + [came]
    else:
        edge = lax.slice_in_dim(vector, size - 1, size, axis=dim)
        came = lax.ppermute(edge, axis, [(i, (i + 1) % count) for i in range(count)])
        rest = [lax.slice_in_dim(vector, 0, size - 1, axis=dim)] if size > 1 else []
        pieces = [came] + rest
    return jnp.concatenate(pieces, axis=dim) if len(pieces) > 1 else pieces[0]


HOPS = (("ta", 1, 1), ("ta", 1, -1), ("xy", 2, 1), ("xy", 2, -1))
LOCAL = ((0, 1), (0, -1), (3, 1), (3, -1))


def neighbours(vector):
    return [shifted(vector, *hop) for hop in HOPS]


def far_products(far, links):
    total = link_product(links[1], far[0], False)
    for number in range(1, 4):
        total = total + link_product(links[number + 1], far[number], False)
    return total


def near_products(rounded, links):
    total = mass_term * rounded.astype(f32) + link_product(links[0], rounded, False)
    for number, (dim, step) in enumerate(LOCAL):
        total = total + link_product(links[number + 5], jnp.roll(rounded, -step, dim), False)
    return total


def sent_adjoint(image, links):
    return [link_product(links[number + 1], image, True).astype(bf16) for number in range(4)]


def near_adjoint(image, links):
    total = mass_term * image.astype(f32) + link_product(links[0], image, True)
    for number, (dim, step) in enumerate(LOCAL):
        term = link_product(links[number + 5], image, True).astype(bf16)
        total = total + jnp.roll(term, step, dim).astype(f32)
    return total


def gram(left, right, precision=None):
    return jnp.einsum("abcdir,abcdit->rt", left, right, precision=precision,
                      preferred_element_type=f32)


def image_gram(full, image):
    low = (full - image.astype(f32)).astype(bf16)
    return gram(image, image) + gram(low, image)


def combine(vector, coefficients):
    return jnp.einsum("abcdir,rt->abcdit", vector, coefficients, precision=lax.Precision.HIGH,
                      preferred_element_type=f32)


def body(sources, links):
    wide = sources.astype(f32)
    far = neighbours(sources)
    near = near_products(sources, links)
    energy = all_sum(gram(sources, sources))
    energy_inv = small(energy_kernel, 1, energy)
    full = near + far_products(far, links)
    image = full.astype(bf16)

    sent = sent_adjoint(image, links)
    full, image, *sent = lax.optimization_barrier((full, image, *sent))
    came = []
    for k, (axis, dim, step) in enumerate(HOPS):
        came.append(shifted(sent[k], axis, dim, -step))
    curvature = all_sum(image_gram(full, image))
    alpha = small(alpha_kernel, 1, curvature, energy)
    normal = near_adjoint(image, links)
    for term in came:
        normal = normal + term.astype(f32)

    normal, rounded = lax.optimization_barrier((normal, normal.astype(bf16)))
    far = neighbours(rounded)
    residual = wide - combine(normal, alpha)
    fresh = gram(residual, residual, lax.Precision.HIGH)
    near = mass_term * (normal - rounded.astype(f32)) + near_products(rounded, links)
    full, normal = lax.optimization_barrier((full, near))
    descent = (full - combine(normal + far_products(far, links), alpha)).astype(bf16)
    square = gram(descent, descent)
    both = all_sum(jnp.concatenate([fresh, square], axis=0), 1)
    size = fresh.shape[0]
    gamma, alpha2 = small(closing_kernel, 2, energy, energy_inv, curvature, alpha, both[:size], both[size:])
    return combine(wide, gamma) + combine(residual, alpha2)


def solution(mesh):
    return jax.shard_map(
        body,
        mesh=mesh,
        in_specs=(
            P("groups", "ta", "xy", None, None, None),
            P("groups", None, "ta", "xy", None, None, None),
        ),
        out_specs=P("groups", "ta", "xy", None, None, None),
        check_vma=False,
    )
```

```python
import functools

import jax
import jax.numpy as jnp
from jax import lax
from jax.experimental import pallas as pl
from jax.experimental.pallas import tpu as pltpu
from jax.sharding import PartitionSpec as P


mass_term = 2.0
MESH = pl.DeviceIdType.MESH
HI = lax.Precision.HIGHEST
f32 = jnp.float32
bf16 = jnp.bfloat16


def sum_kernel(n_ta, n_xy, x_ref, o_ref, parts, whole, send1, recv1, send2, recv2):
    n = n_ta * n_xy
    me = lax.axis_index("ta") * n_xy + lax.axis_index("xy")

    def device(off):
        peer = lax.rem(me + off, n)
        return peer, {"ta": peer // n_xy, "xy": lax.rem(peer, n_xy)}

    def first(off):
        peer, where = device(off)
        return pltpu.make_async_remote_copy(
            src_ref=x_ref.at[peer], dst_ref=parts.at[off], send_sem=send1.at[off],
            recv_sem=recv1.at[off], device_id=where, device_id_type=MESH)

    def second(off):
        _, where = device(off)
        return pltpu.make_async_remote_copy(
            src_ref=whole.at[me], dst_ref=whole.at[me], send_sem=send2.at[off],
            recv_sem=recv2.at[off], device_id=where, device_id_type=MESH)

    def arrived(off):
        peer = lax.rem(me + n - off, n)
        return pltpu.make_async_remote_copy(
            src_ref=whole.at[peer], dst_ref=whole.at[peer], send_sem=send2.at[off],
            recv_sem=recv2.at[off], device_id=device(off)[1], device_id_type=MESH)

    barrier = pltpu.get_barrier_semaphore()

    @pl.loop(1, n)
    def _(off):
        pl.semaphore_signal(barrier, inc=1, device_id=device(off)[1], device_id_type=MESH)

    pl.semaphore_wait(barrier, n - 1)

    @pl.loop(1, n)
    def _(off):
        first(off).start()

    @pl.loop(1, n)
    def _(off):
        first(off).wait_recv()

    acc = x_ref[me]
    for off in range(1, n):
        acc = acc + parts[off]
    whole[me] = acc

    @pl.loop(1, n)
    def _(off):
        second(off).start()

    @pl.loop(1, n)
    def _(off):
        arrived(off).wait_recv()

    o_ref[...] = whole[...]

    @pl.loop(1, n)
    def _(off):
        first(off).wait_send()
        second(off).wait_send()


def all_sum(matrix):
    n_ta, n_xy = lax.axis_size("ta"), lax.axis_size("xy")
    n = n_ta * n_xy
    rows, cols = matrix.shape
    per = -(-rows // n)
    shape = (n, per, cols)
    out = pl.pallas_call(
        functools.partial(sum_kernel, n_ta, n_xy),
        out_shape=jax.ShapeDtypeStruct(shape, f32),
        in_specs=[pl.BlockSpec(memory_space=pltpu.VMEM)],
        out_specs=pl.BlockSpec(memory_space=pltpu.VMEM),
        scratch_shapes=[pltpu.VMEM(shape, f32), pltpu.VMEM(shape, f32)]
        + [pltpu.SemaphoreType.DMA((n,))] * 4,
        cost_estimate=pl.CostEstimate(flops=0, bytes_accessed=64 << 20, transcendentals=0),
        compiler_params=pltpu.CompilerParams(collective_id=0, has_side_effects=True),
    )(jnp.pad(matrix, ((0, per * n - rows), (0, 0))).reshape(shape))
    return out.reshape(n * per, cols)[:rows]


def triangle(n):
    return lax.broadcasted_iota(jnp.int32, (n, n), 0) - lax.broadcasted_iota(jnp.int32, (n, n), 1)


def pack(first, second):
    n = first.shape[0]
    where = triangle(n)
    diag = jnp.sum(jnp.where(where == 0, second, 0.0), axis=0, keepdims=True)
    return jnp.concatenate([jnp.where(where >= 0, first, second), diag], axis=0)


def unpack(ref):
    n = ref.shape[1]
    where = triangle(n)
    both = ref[:n, :]
    turned = both.T
    first = jnp.where(where >= 0, both, turned)
    second = jnp.where(where < 0, both, turned)
    return first, jnp.where(where == 0, ref[n:n + 1, :], second)


dot = functools.partial(jnp.dot, precision=HI, preferred_element_type=f32)


def dot_t(a, b):
    return lax.dot_general(a, b, (((0,), (0,)), ((), ())), precision=HI, preferred_element_type=f32)


def symmetric(a):
    return 0.5 * (a + a.T)


def invert(a, x_ref, s_ref):
    n = a.shape[0]
    row = lax.broadcasted_iota(jnp.int32, (n, n), 0)
    col = lax.broadcasted_iota(jnp.int32, (n, n), 1)
    eye = jnp.where(row == col, 1.0, 0.0).astype(f32)
    diag = a * eye
    down = lax.rsqrt(jnp.sum(diag, axis=1, keepdims=True))
    across = lax.rsqrt(jnp.sum(diag, axis=0, keepdims=True))
    a = a * down * across
    s_ref[...] = a
    power = eye - a
    x = eye + power
    for _ in range(3):
        power = dot(power, power)
        x = x + dot(x, power)
    x_ref[...] = x
    worst = jnp.max(jnp.abs(eye - dot(a, x)))

    @pl.when(jnp.logical_not(worst < 1e-3))
    def _():
        x_ref[...] = s_ref[...]

        def eliminate(k, carry):
            m = x_ref[...]
            pivot_row = x_ref[pl.ds(k, 1), :]
            here = col == k
            pivot_col = jnp.sum(jnp.where(here, m, 0.0), axis=1, keepdims=True)
            hit = here[:1]
            inv = 1.0 / jnp.sum(jnp.where(hit, pivot_row, 0.0), axis=1, keepdims=True)
            scaled = jnp.where(hit, inv, pivot_row * inv)
            m = jnp.where(here, 0.0, m) - pivot_col * scaled
            x_ref[...] = jnp.where(row == k, scaled, m)
            return carry

        lax.fori_loop(0, n, eliminate, 0)

    x = x_ref[...]
    x = x + dot(x, eye - dot(s_ref[...], x))
    return x * down * across


def solved(a, inverse, right):
    out = dot(inverse, right)
    return out + dot(inverse, right - dot(a, out))


def alpha_kernel(both_ref, o_ref, x_ref, s_ref):
    energy, curvature = unpack(both_ref)
    inverse = invert(curvature, x_ref, s_ref)
    o_ref[...] = solved(curvature, inverse, energy)


def energy_kernel(both_ref, o_ref, x_ref, s_ref):
    o_ref[...] = invert(unpack(both_ref)[0], x_ref, s_ref)


def closing_kernel(both_ref, inverse_ref, alpha_ref, late_ref, gamma_ref, alpha2_ref, x_ref, s_ref):
    energy, curvature = unpack(both_ref)
    fresh, square = unpack(late_ref)
    beta = solved(energy, inverse_ref[...], fresh)
    second = symmetric(square - dot_t(beta, dot(curvature, beta)))
    inverse = invert(second, x_ref, s_ref)
    alpha2 = solved(second, inverse, fresh)
    alpha2_ref[...] = alpha2
    gamma_ref[...] = alpha_ref[...] + dot(beta, alpha2)


def small(kernel, count, *args):
    spec = pl.BlockSpec(memory_space=pltpu.VMEM)
    shape = (args[0].shape[1],) * 2
    out = pl.pallas_call(
        kernel,
        out_shape=[jax.ShapeDtypeStruct(shape, f32)] * count,
        in_specs=[spec] * len(args),
        out_specs=[spec] * count,
        scratch_shapes=[pltpu.VMEM(shape, f32)] * 2,
        cost_estimate=pl.CostEstimate(flops=int(4e9), bytes_accessed=1 << 20, transcendentals=0),
    )(*args)
    return out if count > 1 else out[0]


def link_product(link_field, vector, flipped):
    einsum_form = "abcdio,abcdir->abcdor" if flipped else "abcdoi,abcdir->abcdor"
    return jnp.einsum(einsum_form, link_field, vector, preferred_element_type=f32)


def shifted(vector, axis, dim, step):
    count, size = lax.axis_size(axis), vector.shape[dim]
    if step > 0:
        edge = lax.slice_in_dim(vector, 0, 1, axis=dim)
        came = lax.ppermute(edge, axis, [((i + 1) % count, i) for i in range(count)])
        rest = [lax.slice_in_dim(vector, 1, size, axis=dim)] if size > 1 else []
        pieces = rest + [came]
    else:
        edge = lax.slice_in_dim(vector, size - 1, size, axis=dim)
        came = lax.ppermute(edge, axis, [(i, (i + 1) % count) for i in range(count)])
        rest = [lax.slice_in_dim(vector, 0, size - 1, axis=dim)] if size > 1 else []
        pieces = [came] + rest
    return jnp.concatenate(pieces, axis=dim) if len(pieces) > 1 else pieces[0]


HOPS = (("ta", 1, 1), ("ta", 1, -1), ("xy", 2, 1), ("xy", 2, -1))
LOCAL = ((0, 1), (0, -1), (3, 1), (3, -1))


def neighbours(vector):
    return [shifted(vector, *hop) for hop in HOPS]


def hop_products(numbers, far, links):
    return sum(link_product(links[number + 1], far[number], False) for number in numbers)


def fold_kernel(sites, near_ref, plus_ref, minus_ref, lp_ref, lm_ref, y_ref, image_ref, up_ref, um_ref):
    mul = functools.partial(lax.dot_general, preferred_element_type=f32)
    straight, turned = (((1,), (0,)), ((), ())), (((0,), (0,)), ((), ()))
    for s in range(sites):
        plus, minus = lp_ref[0, s], lm_ref[0, s]
        y = near_ref[s] + mul(plus, plus_ref[s], straight) + mul(minus, minus_ref[s], straight)
        image = y.astype(bf16)
        y_ref[s] = y
        image_ref[s] = image
        up_ref[s] = mul(plus, image, turned).astype(bf16)
        um_ref[s] = mul(minus, image, turned).astype(bf16)


def fold(near, plus, minus, links):
    shape = near.shape
    total, (o, r), i = near.size // (shape[-1] * shape[-2]), shape[-2:], links.shape[-1]
    sites = shape[3]
    vec = pl.BlockSpec((sites, o, r), lambda g: (g, 0, 0))
    flat = lambda v: v.reshape(total, o, r)
    whole = links.reshape(links.shape[0], total, o, i)
    outs = pl.pallas_call(
        functools.partial(fold_kernel, sites),
        grid=(total // sites,),
        out_shape=[jax.ShapeDtypeStruct((total, o, r), d) for d in (f32, bf16, bf16, bf16)],
        in_specs=[vec, vec, vec] + [pl.BlockSpec((1, sites, o, i), lambda g, k=k: (k, g, 0, 0)) for k in (3, 4)],
        out_specs=[vec] * 4,
        cost_estimate=pl.CostEstimate(flops=int(2e9), bytes_accessed=20 << 20, transcendentals=0),
    )(flat(near), flat(plus), flat(minus), whole, whole)
    return [v.reshape(shape) for v in outs]


def near_products(rounded, links):
    total = mass_term * rounded.astype(f32) + link_product(links[0], rounded, False)
    for number, (dim, step) in enumerate(LOCAL):
        total = total + link_product(links[number + 5], jnp.roll(rounded, -step, dim), False)
    return total


def near_adjoint(image, links):
    total = mass_term * image.astype(f32) + link_product(links[0], image, True)
    for number, (dim, step) in enumerate(LOCAL):
        term = link_product(links[number + 5], image, True).astype(bf16)
        total = total + jnp.roll(term, step, dim).astype(f32)
    return total


def gram(left, right, precision=None):
    return jnp.einsum("abcdir,abcdit->rt", left, right, precision=precision,
                      preferred_element_type=f32)


def image_gram(full, image):
    low = (full - image.astype(f32)).astype(bf16)
    return gram(image, image) + gram(low, image)


def combine(vector, coefficients):
    return jnp.einsum("abcdir,rt->abcdit", vector, coefficients, precision=lax.Precision.HIGH,
                      preferred_element_type=f32)


def body(sources, links):
    wide = sources.astype(f32)
    far = neighbours(sources)
    near = near_products(sources, links) + hop_products((0, 1), far, links)
    energy = gram(sources, sources)
    full, image, *along = fold(near, far[2], far[3], links)
    sent = [link_product(links[k + 1], image, True).astype(bf16) for k in range(2)] + along
    full, image, *sent = lax.optimization_barrier((full, image, *sent))
    came = []
    for k, (axis, dim, step) in enumerate(HOPS):
        came.append(shifted(sent[k], axis, dim, -step))
    early = all_sum(pack(energy, symmetric(image_gram(full, image))))
    normal = near_adjoint(image, links)
    for term in came:
        normal = normal + term.astype(f32)

    normal, rounded = lax.optimization_barrier((normal, normal.astype(bf16)))
    far = []
    for hop in HOPS:
        far.append(shifted(rounded, *hop))
    alpha = small(alpha_kernel, 1, early)
    energy_inv = small(energy_kernel, 1, early)
    residual = wide - combine(normal, alpha)
    fresh = gram(residual, residual, lax.Precision.HIGH)
    near = mass_term * (normal - rounded.astype(f32)) + near_products(rounded, links)
    full, normal = lax.optimization_barrier((full, near))
    normal = normal + hop_products((0, 1), far, links) + hop_products((2, 3), far, links)
    descent = (full - combine(normal, alpha)).astype(bf16)
    late = all_sum(pack(fresh, gram(descent, descent)))
    gamma, alpha2 = small(closing_kernel, 2, early, energy_inv, alpha, late)
    return combine(wide, gamma) + combine(residual, alpha2)


def solution(mesh):
    return jax.shard_map(
        body,
        mesh=mesh,
        in_specs=(
            P("groups", "ta", "xy", None, None, None),
            P("groups", None, "ta", "xy", None, None, None),
        ),
        out_specs=P("groups", "ta", "xy", None, None, None),
        check_vma=False,
    )
```

```python
import functools

import jax
import jax.numpy as jnp
from jax import lax
from jax.experimental import pallas as pl
from jax.experimental.pallas import tpu as pltpu
from jax.sharding import PartitionSpec as P


mass_term = 2.0
MESH = pl.DeviceIdType.MESH
HI = lax.Precision.HIGHEST
f32 = jnp.float32
bf16 = jnp.bfloat16


def sum_kernel(n_ta, n_xy, x_ref, d_ref, o_ref, p_ref, parts, whole, dparts, dwhole, send1, recv1, send2, recv2):
    n = n_ta * n_xy
    me = lax.axis_index("ta") * n_xy + lax.axis_index("xy")

    def device(off):
        peer = lax.rem(me + off, n)
        return peer, {"ta": peer // n_xy, "xy": lax.rem(peer, n_xy)}

    def copies(off, pairs, send, recv):
        return [pltpu.make_async_remote_copy(
            src_ref=src, dst_ref=dst, send_sem=send.at[k, off], recv_sem=recv.at[k, off],
            device_id=device(off)[1], device_id_type=MESH) for k, (src, dst) in enumerate(pairs)]

    def first(off):
        peer = device(off)[0]
        return copies(off, ((x_ref.at[peer], parts.at[off]), (d_ref.at[peer], dparts.at[off])), send1, recv1)

    def second(off, owner):
        return copies(off, ((whole.at[owner], whole.at[owner]), (dwhole.at[owner], dwhole.at[owner])), send2, recv2)

    barrier = pltpu.get_barrier_semaphore()

    @pl.loop(1, n)
    def _(off):
        pl.semaphore_signal(barrier, inc=1, device_id=device(off)[1], device_id_type=MESH)

    pl.semaphore_wait(barrier, n - 1)

    @pl.loop(1, n)
    def _(off):
        for copy in first(off):
            copy.start()

    @pl.loop(1, n)
    def _(off):
        for copy in first(off):
            copy.wait_recv()

    acc, dacc = x_ref[me], d_ref[me]
    for off in range(1, n):
        acc = acc + parts[off]
        dacc = dacc + dparts[off]
    whole[me] = acc
    dwhole[me] = dacc

    @pl.loop(1, n)
    def _(off):
        for copy in second(off, me):
            copy.start()

    @pl.loop(1, n)
    def _(off):
        for copy in second(off, lax.rem(me + n - off, n)):
            copy.wait_recv()

    o_ref[...] = whole[...]
    p_ref[...] = dwhole[...]

    @pl.loop(1, n)
    def _(off):
        for copy in first(off) + second(off, me):
            copy.wait_send()


def all_sum(matrix, diag):
    n_ta, n_xy = lax.axis_size("ta"), lax.axis_size("xy")
    n = n_ta * n_xy
    rows, cols = matrix.shape
    per = -(-rows // n)
    shape = (n, per, cols)
    lanes = -(-per // 128) * 128
    side = (n, 1, lanes)
    spec = pl.BlockSpec(memory_space=pltpu.VMEM)
    filled = jnp.pad(matrix, ((0, per * n - rows), (0, 0))) if per * n != rows else matrix
    diags = jnp.pad(jnp.pad(diag, (0, per * n - rows)).reshape(n, 1, per), ((0, 0), (0, 0), (0, lanes - per)))
    out, dout = pl.pallas_call(
        functools.partial(sum_kernel, n_ta, n_xy),
        out_shape=[jax.ShapeDtypeStruct(shape, f32), jax.ShapeDtypeStruct(side, f32)],
        in_specs=[spec] * 2,
        out_specs=[spec] * 2,
        scratch_shapes=[pltpu.VMEM(shape, f32)] * 2 + [pltpu.VMEM(side, f32)] * 2
        + [pltpu.SemaphoreType.DMA((2, n))] * 4,
        cost_estimate=pl.CostEstimate(flops=0, bytes_accessed=64 << 20, transcendentals=0),
        compiler_params=pltpu.CompilerParams(collective_id=0, has_side_effects=True),
    )(filled.reshape(shape), diags)
    return out.reshape(n * per, cols)[:rows], dout[:, 0, :per].reshape(1, n * per)[:, :rows]


def triangle(n):
    return lax.broadcasted_iota(jnp.int32, (n, n), 0) - lax.broadcasted_iota(jnp.int32, (n, n), 1)


def sum_pair(first, second):
    where = triangle(first.shape[0])
    diag = jnp.sum(jnp.where(where == 0, second, 0.0), axis=0)
    return all_sum(jnp.where(where >= 0, first, second), diag)


def unpack(ref, diag_ref):
    both = ref[...]
    where = triangle(both.shape[0])
    turned = both.T
    first = jnp.where(where >= 0, both, turned)
    second = jnp.where(where < 0, both, turned)
    return first, jnp.where(where == 0, diag_ref[...], second)


dot = functools.partial(jnp.dot, precision=HI, preferred_element_type=f32)


def dot_t(a, b):
    return lax.dot_general(a, b, (((0,), (0,)), ((), ())), precision=HI, preferred_element_type=f32)


def symmetric(a):
    return 0.5 * (a + a.T)


def invert(a, x_ref, s_ref):
    n = a.shape[0]
    row = lax.broadcasted_iota(jnp.int32, (n, n), 0)
    col = lax.broadcasted_iota(jnp.int32, (n, n), 1)
    eye = jnp.where(row == col, 1.0, 0.0).astype(f32)
    diag = a * eye
    down = lax.rsqrt(jnp.sum(diag, axis=1, keepdims=True))
    across = lax.rsqrt(jnp.sum(diag, axis=0, keepdims=True))
    a = a * down * across
    s_ref[...] = a
    power = eye - a
    x = eye + power
    for _ in range(3):
        power = dot(power, power)
        x = x + dot(x, power)
    x_ref[...] = x
    worst = jnp.max(jnp.abs(eye - dot(a, x)))

    @pl.when(jnp.logical_not(worst < 1e-3))
    def _():
        x_ref[...] = s_ref[...]

        def eliminate(k, carry):
            m = x_ref[...]
            pivot_row = x_ref[pl.ds(k, 1), :]
            here = col == k
            pivot_col = jnp.sum(jnp.where(here, m, 0.0), axis=1, keepdims=True)
            hit = here[:1]
            inv = 1.0 / jnp.sum(jnp.where(hit, pivot_row, 0.0), axis=1, keepdims=True)
            scaled = jnp.where(hit, inv, pivot_row * inv)
            m = jnp.where(here, 0.0, m) - pivot_col * scaled
            x_ref[...] = jnp.where(row == k, scaled, m)
            return carry

        lax.fori_loop(0, n, eliminate, 0)

    x = x_ref[...]
    x = x + dot(x, eye - dot(s_ref[...], x))
    return x * down * across


def solved(a, inverse, right):
    out = dot(inverse, right)
    return out + dot(inverse, right - dot(a, out))


def alpha_kernel(both_ref, diag_ref, o_ref, x_ref, s_ref):
    energy, curvature = unpack(both_ref, diag_ref)
    inverse = invert(curvature, x_ref, s_ref)
    o_ref[...] = solved(curvature, inverse, energy)


def energy_kernel(both_ref, diag_ref, o_ref, x_ref, s_ref):
    o_ref[...] = invert(unpack(both_ref, diag_ref)[0], x_ref, s_ref)


def closing_kernel(both_ref, diag_ref, inverse_ref, alpha_ref, late_ref, late_diag_ref, gamma_ref, alpha2_ref,
                   x_ref, s_ref):
    energy, curvature = unpack(both_ref, diag_ref)
    fresh, square = unpack(late_ref, late_diag_ref)
    beta = solved(energy, inverse_ref[...], fresh)
    second = symmetric(square - dot_t(beta, dot(curvature, beta)))
    inverse = invert(second, x_ref, s_ref)
    alpha2 = solved(second, inverse, fresh)
    alpha2_ref[...] = alpha2
    gamma_ref[...] = alpha_ref[...] + dot(beta, alpha2)


def small(kernel, count, *args):
    spec = pl.BlockSpec(memory_space=pltpu.VMEM)
    shape = (args[0].shape[1],) * 2
    out = pl.pallas_call(
        kernel,
        out_shape=[jax.ShapeDtypeStruct(shape, f32)] * count,
        in_specs=[spec] * len(args),
        out_specs=[spec] * count,
        scratch_shapes=[pltpu.VMEM(shape, f32)] * 2,
        cost_estimate=pl.CostEstimate(flops=int(4e9), bytes_accessed=1 << 20, transcendentals=0),
    )(*args)
    return out if count > 1 else out[0]


def link_product(link_field, vector, flipped):
    einsum_form = "abcdio,abcdir->abcdor" if flipped else "abcdoi,abcdir->abcdor"
    return jnp.einsum(einsum_form, link_field, vector, preferred_element_type=f32)


def shifted(vector, axis, dim, step):
    count, size = lax.axis_size(axis), vector.shape[dim]
    if step > 0:
        edge = lax.slice_in_dim(vector, 0, 1, axis=dim)
        came = lax.ppermute(edge, axis, [((i + 1) % count, i) for i in range(count)])
        rest = [lax.slice_in_dim(vector, 1, size, axis=dim)] if size > 1 else []
        pieces = rest + [came]
    else:
        edge = lax.slice_in_dim(vector, size - 1, size, axis=dim)
        came = lax.ppermute(edge, axis, [(i, (i + 1) % count) for i in range(count)])
        rest = [lax.slice_in_dim(vector, 0, size - 1, axis=dim)] if size > 1 else []
        pieces = [came] + rest
    return jnp.concatenate(pieces, axis=dim) if len(pieces) > 1 else pieces[0]


HOPS = (("ta", 1, 1), ("ta", 1, -1), ("xy", 2, 1), ("xy", 2, -1))
LOCAL = ((0, 1), (0, -1), (3, 1), (3, -1))


def neighbours(vector):
    return [shifted(vector, *hop) for hop in HOPS]


def hop_products(numbers, far, links):
    return sum(link_product(links[number + 1], far[number], False) for number in numbers)


def fold_kernel(sites, near_ref, plus_ref, minus_ref, l1_ref, l2_ref, lp_ref, lm_ref, y_ref, image_ref, *u_refs):
    mul = functools.partial(lax.dot_general, preferred_element_type=f32)
    straight, turned = (((1,), (0,)), ((), ())), (((0,), (0,)), ((), ()))
    for s in range(sites):
        plus, minus = lp_ref[0, s], lm_ref[0, s]
        y = near_ref[s] + mul(plus, plus_ref[s], straight) + mul(minus, minus_ref[s], straight)
        image = y.astype(bf16)
        y_ref[s] = y
        image_ref[s] = image
        for link, u_ref in zip((l1_ref[0, s], l2_ref[0, s], plus, minus), u_refs):
            u_ref[s] = mul(link, image, turned).astype(bf16)


def fold(near, plus, minus, links):
    shape = near.shape
    total, (o, r), i = near.size // (shape[-1] * shape[-2]), shape[-2:], links.shape[-1]
    sites = shape[3]
    vec = pl.BlockSpec((sites, o, r), lambda g: (g, 0, 0))
    flat = lambda v: v.reshape(total, o, r)
    whole = links.reshape(links.shape[0], total, o, i)
    outs = pl.pallas_call(
        functools.partial(fold_kernel, sites),
        grid=(total // sites,),
        out_shape=[jax.ShapeDtypeStruct((total, o, r), d) for d in (f32,) + (bf16,) * 5],
        in_specs=[vec, vec, vec] + [pl.BlockSpec((1, sites, o, i), lambda g, k=k: (k, g, 0, 0)) for k in (1, 2, 3, 4)],
        out_specs=[vec] * 6,
        cost_estimate=pl.CostEstimate(flops=int(2e9), bytes_accessed=20 << 20, transcendentals=0),
    )(flat(near), flat(plus), flat(minus), *[whole] * 4)
    return [v.reshape(shape) for v in outs]


def near_products(rounded, links):
    total = mass_term * rounded.astype(f32) + link_product(links[0], rounded, False)
    for number, (dim, step) in enumerate(LOCAL):
        total = total + link_product(links[number + 5], jnp.roll(rounded, -step, dim), False)
    return total


def near_adjoint(image, links):
    total = mass_term * image.astype(f32) + link_product(links[0], image, True)
    for number, (dim, step) in enumerate(LOCAL):
        term = link_product(links[number + 5], image, True).astype(bf16)
        total = total + jnp.roll(term, step, dim).astype(f32)
    return total


def gram(left, right, precision=None):
    return jnp.einsum("abcdir,abcdit->rt", left, right, precision=precision,
                      preferred_element_type=f32)


def image_gram(full, image):
    low = (full - image.astype(f32)).astype(bf16)
    return gram(image, image) + gram(low, image)


def combine(vector, coefficients):
    return jnp.einsum("abcdir,rt->abcdit", vector, coefficients, precision=lax.Precision.HIGH,
                      preferred_element_type=f32)


def body(sources, links):
    wide = sources.astype(f32)
    far = neighbours(sources)
    near = near_products(sources, links) + hop_products((0, 1), far, links)
    energy = gram(sources, sources)
    full, image, *sent = fold(near, far[2], far[3], links)
    full, image, *sent = lax.optimization_barrier((full, image, *sent))
    came = []
    for k, (axis, dim, step) in enumerate(HOPS):
        came.append(shifted(sent[k], axis, dim, -step))
    squares = symmetric(image_gram(full, image))
    early = sum_pair(energy, squares)
    normal = near_adjoint(image, links)
    for term in came:
        normal = normal + term.astype(f32)

    normal, rounded = lax.optimization_barrier((normal, normal.astype(bf16)))
    far = []
    for hop in HOPS:
        far.append(shifted(rounded, *hop))
    alpha = small(alpha_kernel, 1, *early)
    energy_inv = small(energy_kernel, 1, *early)
    residual = wide - combine(normal, alpha)
    fresh = gram(residual, residual, lax.Precision.HIGH)
    rounded, normal_late, _ = lax.optimization_barrier((rounded, normal, energy_inv))
    near = mass_term * (normal_late - rounded.astype(f32)) + near_products(rounded, links)
    full, normal = lax.optimization_barrier((full, near))
    normal = normal + hop_products((0, 1), far, links) + hop_products((2, 3), far, links)
    descent = (full - combine(normal, alpha)).astype(bf16)
    late = sum_pair(fresh, gram(descent, descent))
    gamma, alpha2 = small(closing_kernel, 2, *early, energy_inv, alpha, *late)
    return combine(wide, gamma) + combine(residual, alpha2)


def solution(mesh):
    return jax.shard_map(
        body,
        mesh=mesh,
        in_specs=(
            P("groups", "ta", "xy", None, None, None),
            P("groups", None, "ta", "xy", None, None, None),
        ),
        out_specs=P("groups", "ta", "xy", None, None, None),
        check_vma=False,
    )
```

```python
import functools

import jax
import jax.numpy as jnp
from jax import lax
from jax.experimental import pallas as pl
from jax.experimental.pallas import tpu as pltpu
from jax.sharding import PartitionSpec as P


mass_term = 2.0
MESH = pl.DeviceIdType.MESH
HI = lax.Precision.HIGHEST
f32 = jnp.float32
bf16 = jnp.bfloat16


def sum_kernel(n_ta, n_xy, x_ref, d_ref, o_ref, p_ref, parts, whole, dparts, dwhole, send1, recv1, send2, recv2):
    n = n_ta * n_xy
    me = lax.axis_index("ta") * n_xy + lax.axis_index("xy")

    def device(off):
        peer = lax.rem(me + off, n)
        return peer, {"ta": peer // n_xy, "xy": lax.rem(peer, n_xy)}

    def copies(off, pairs, send, recv):
        return [pltpu.make_async_remote_copy(
            src_ref=src, dst_ref=dst, send_sem=send.at[k, off], recv_sem=recv.at[k, off],
            device_id=device(off)[1], device_id_type=MESH) for k, (src, dst) in enumerate(pairs)]

    def first(off):
        peer = device(off)[0]
        return copies(off, ((x_ref.at[peer], parts.at[off]), (d_ref.at[peer], dparts.at[off])), send1, recv1)

    def second(off, owner):
        return copies(off, ((whole.at[owner], whole.at[owner]), (dwhole.at[owner], dwhole.at[owner])), send2, recv2)

    barrier = pltpu.get_barrier_semaphore()

    @pl.loop(1, n)
    def _(off):
        pl.semaphore_signal(barrier, inc=1, device_id=device(off)[1], device_id_type=MESH)

    pl.semaphore_wait(barrier, n - 1)

    @pl.loop(1, n)
    def _(off):
        for copy in first(off):
            copy.start()

    @pl.loop(1, n)
    def _(off):
        for copy in first(off):
            copy.wait_recv()

    acc, dacc = x_ref[me], d_ref[me]
    for off in range(1, n):
        acc = acc + parts[off]
        dacc = dacc + dparts[off]
    whole[me] = acc
    dwhole[me] = dacc

    @pl.loop(1, n)
    def _(off):
        for copy in second(off, me):
            copy.start()

    @pl.loop(1, n)
    def _(off):
        for copy in second(off, lax.rem(me + n - off, n)):
            copy.wait_recv()

    o_ref[...] = whole[...]
    p_ref[...] = dwhole[...]

    @pl.loop(1, n)
    def _(off):
        for copy in first(off) + second(off, me):
            copy.wait_send()


def all_sum(matrix, diag):
    n_ta, n_xy = lax.axis_size("ta"), lax.axis_size("xy")
    n = n_ta * n_xy
    rows, cols = matrix.shape
    per = -(-rows // n)
    shape = (n, per, cols)
    lanes = -(-per // 128) * 128
    side = (n, 1, lanes)
    spec = pl.BlockSpec(memory_space=pltpu.VMEM)
    filled = jnp.pad(matrix, ((0, per * n - rows), (0, 0))) if per * n != rows else matrix
    diags = jnp.pad(jnp.pad(diag, (0, per * n - rows)).reshape(n, 1, per), ((0, 0), (0, 0), (0, lanes - per)))
    out, dout = pl.pallas_call(
        functools.partial(sum_kernel, n_ta, n_xy),
        out_shape=[jax.ShapeDtypeStruct(shape, f32), jax.ShapeDtypeStruct(side, f32)],
        in_specs=[spec] * 2,
        out_specs=[spec] * 2,
        scratch_shapes=[pltpu.VMEM(shape, f32)] * 2 + [pltpu.VMEM(side, f32)] * 2
        + [pltpu.SemaphoreType.DMA((2, n))] * 4,
        cost_estimate=pl.CostEstimate(flops=0, bytes_accessed=64 << 20, transcendentals=0),
        compiler_params=pltpu.CompilerParams(collective_id=0, has_side_effects=True),
    )(filled.reshape(shape), diags)
    return out.reshape(n * per, cols)[:rows], dout[:, 0, :per].reshape(1, n * per)[:, :rows]


def triangle(n):
    return lax.broadcasted_iota(jnp.int32, (n, n), 0) - lax.broadcasted_iota(jnp.int32, (n, n), 1)


def sum_pair(first, second):
    where = triangle(first.shape[0])
    diag = jnp.sum(jnp.where(where == 0, second, 0.0), axis=0)
    return all_sum(jnp.where(where >= 0, first, second), diag)


def unpack(ref, diag_ref):
    both = ref[...]
    where = triangle(both.shape[0])
    turned = both.T
    first = jnp.where(where >= 0, both, turned)
    second = jnp.where(where < 0, both, turned)
    return first, jnp.where(where == 0, diag_ref[...], second)


dot = functools.partial(jnp.dot, precision=HI, preferred_element_type=f32)


def dot_t(a, b):
    return lax.dot_general(a, b, (((0,), (0,)), ((), ())), precision=HI, preferred_element_type=f32)


def symmetric(a):
    return 0.5 * (a + a.T)


def invert(a, x_ref, s_ref, p_ref):
    n = a.shape[0]
    row = lax.broadcasted_iota(jnp.int32, (n, n), 0)
    col = lax.broadcasted_iota(jnp.int32, (n, n), 1)
    eye = jnp.where(row == col, 1.0, 0.0).astype(f32)
    diag = a * eye
    down = lax.rsqrt(jnp.sum(diag, axis=1, keepdims=True))
    across = lax.rsqrt(jnp.sum(diag, axis=0, keepdims=True))
    a = a * down * across
    s_ref[...] = a
    p_ref[...] = eye - a
    x_ref[...] = eye + p_ref[...]

    def square(_, carry):
        power = dot(p_ref[...], p_ref[...])
        p_ref[...] = power
        x_ref[...] = x_ref[...] + dot(x_ref[...], power)
        return carry

    lax.fori_loop(0, 3, square, 0)
    worst = jnp.max(jnp.abs(eye - dot(a, x_ref[...])))

    @pl.when(jnp.logical_not(worst < 1e-3))
    def _():
        x_ref[...] = s_ref[...]

        def eliminate(k, carry):
            m = x_ref[...]
            pivot_row = x_ref[pl.ds(k, 1), :]
            here = col == k
            pivot_col = jnp.sum(jnp.where(here, m, 0.0), axis=1, keepdims=True)
            hit = here[:1]
            inv = 1.0 / jnp.sum(jnp.where(hit, pivot_row, 0.0), axis=1, keepdims=True)
            scaled = jnp.where(hit, inv, pivot_row * inv)
            m = jnp.where(here, 0.0, m) - pivot_col * scaled
            x_ref[...] = jnp.where(row == k, scaled, m)
            return carry

        lax.fori_loop(0, n, eliminate, 0)

    x = x_ref[...]
    x = x + dot(x, eye - dot(s_ref[...], x))
    return x * down * across


def solved(a, inverse, right):
    out = dot(inverse, right)
    return out + dot(inverse, right - dot(a, out))


def alpha_kernel(both_ref, diag_ref, o_ref, x_ref, s_ref, p_ref):
    energy, curvature = unpack(both_ref, diag_ref)
    inverse = invert(curvature, x_ref, s_ref, p_ref)
    o_ref[...] = solved(curvature, inverse, energy)


def energy_kernel(both_ref, diag_ref, o_ref, x_ref, s_ref, p_ref):
    o_ref[...] = invert(unpack(both_ref, diag_ref)[0], x_ref, s_ref, p_ref)


def closing_kernel(both_ref, diag_ref, inverse_ref, alpha_ref, late_ref, late_diag_ref, gamma_ref, alpha2_ref,
                   x_ref, s_ref, p_ref):
    energy, curvature = unpack(both_ref, diag_ref)
    fresh, square = unpack(late_ref, late_diag_ref)
    beta = solved(energy, inverse_ref[...], fresh)
    second = symmetric(square - dot_t(beta, dot(curvature, beta)))
    inverse = invert(second, x_ref, s_ref, p_ref)
    alpha2 = solved(second, inverse, fresh)
    alpha2_ref[...] = alpha2
    gamma_ref[...] = alpha_ref[...] + dot(beta, alpha2)


def small(kernel, count, *args):
    spec = pl.BlockSpec(memory_space=pltpu.VMEM)
    shape = (args[0].shape[1],) * 2
    out = pl.pallas_call(
        kernel,
        out_shape=[jax.ShapeDtypeStruct(shape, f32)] * count,
        in_specs=[spec] * len(args),
        out_specs=[spec] * count,
        scratch_shapes=[pltpu.VMEM(shape, f32)] * 3,
        cost_estimate=pl.CostEstimate(flops=int(4e9), bytes_accessed=1 << 20, transcendentals=0),
    )(*args)
    return out if count > 1 else out[0]


def link_product(link_field, vector, flipped):
    einsum_form = "abcdio,abcdir->abcdor" if flipped else "abcdoi,abcdir->abcdor"
    return jnp.einsum(einsum_form, link_field, vector, preferred_element_type=f32)


def shifted(vector, axis, dim, step):
    count, size = lax.axis_size(axis), vector.shape[dim]
    if step > 0:
        edge = lax.slice_in_dim(vector, 0, 1, axis=dim)
        came = lax.ppermute(edge, axis, [((i + 1) % count, i) for i in range(count)])
        rest = [lax.slice_in_dim(vector, 1, size, axis=dim)] if size > 1 else []
        pieces = rest + [came]
    else:
        edge = lax.slice_in_dim(vector, size - 1, size, axis=dim)
        came = lax.ppermute(edge, axis, [(i, (i + 1) % count) for i in range(count)])
        rest = [lax.slice_in_dim(vector, 0, size - 1, axis=dim)] if size > 1 else []
        pieces = [came] + rest
    return jnp.concatenate(pieces, axis=dim) if len(pieces) > 1 else pieces[0]


HOPS = (("ta", 1, 1), ("ta", 1, -1), ("xy", 2, 1), ("xy", 2, -1))
LOCAL = ((0, 1), (0, -1), (3, 1), (3, -1))


def neighbours(vector):
    return [shifted(vector, *hop) for hop in HOPS]


def hop_products(numbers, far, links):
    return sum(link_product(links[number + 1], far[number], False) for number in numbers)


def fold_kernel(sites, near_ref, plus_ref, minus_ref, l1_ref, l2_ref, lp_ref, lm_ref, y_ref, image_ref, *u_refs):
    mul = functools.partial(lax.dot_general, preferred_element_type=f32)
    straight, turned = (((1,), (0,)), ((), ())), (((0,), (0,)), ((), ()))
    for s in range(sites):
        plus, minus = lp_ref[0, s], lm_ref[0, s]
        y = near_ref[s] + mul(plus, plus_ref[s], straight) + mul(minus, minus_ref[s], straight)
        image = y.astype(bf16)
        y_ref[s] = y
        image_ref[s] = image
        for link, u_ref in zip((l1_ref[0, s], l2_ref[0, s], plus, minus), u_refs):
            u_ref[s] = mul(link, image, turned).astype(bf16)


def fold(near, plus, minus, links):
    shape = near.shape
    total, (o, r), i = near.size // (shape[-1] * shape[-2]), shape[-2:], links.shape[-1]
    sites = shape[3]
    vec = pl.BlockSpec((sites, o, r), lambda g: (g, 0, 0))
    flat = lambda v: v.reshape(total, o, r)
    whole = links.reshape(links.shape[0], total, o, i)
    outs = pl.pallas_call(
        functools.partial(fold_kernel, sites),
        grid=(total // sites,),
        out_shape=[jax.ShapeDtypeStruct((total, o, r), d) for d in (f32,) + (bf16,) * 5],
        in_specs=[vec, vec, vec] + [pl.BlockSpec((1, sites, o, i), lambda g, k=k: (k, g, 0, 0)) for k in (1, 2, 3, 4)],
        out_specs=[vec] * 6,
        cost_estimate=pl.CostEstimate(flops=int(2e9), bytes_accessed=20 << 20, transcendentals=0),
    )(flat(near), flat(plus), flat(minus), *[whole] * 4)
    return [v.reshape(shape) for v in outs]


def near_products(rounded, links):
    total = mass_term * rounded.astype(f32) + link_product(links[0], rounded, False)
    for number, (dim, step) in enumerate(LOCAL):
        total = total + link_product(links[number + 5], jnp.roll(rounded, -step, dim), False)
    return total


def near_adjoint(image, links):
    total = mass_term * image.astype(f32) + link_product(links[0], image, True)
    for number, (dim, step) in enumerate(LOCAL):
        term = link_product(links[number + 5], image, True).astype(bf16)
        total = total + jnp.roll(term, step, dim).astype(f32)
    return total


def gram(left, right, precision=None):
    return jnp.einsum("abcdir,abcdit->rt", left, right, precision=precision,
                      preferred_element_type=f32)


def image_gram(full, image):
    low = (full - image.astype(f32)).astype(bf16)
    return gram(image, image) + gram(low, image)


def combine(vector, coefficients):
    return jnp.einsum("abcdir,rt->abcdit", vector, coefficients, precision=lax.Precision.HIGH,
                      preferred_element_type=f32)


def body(sources, links):
    wide = sources.astype(f32)
    far = neighbours(sources)
    near = near_products(sources, links) + hop_products((0, 1), far, links)
    energy = gram(sources, sources)
    full, image, *sent = fold(near, far[2], far[3], links)
    full, image, *sent = lax.optimization_barrier((full, image, *sent))
    came = []
    for k, (axis, dim, step) in enumerate(HOPS):
        came.append(shifted(sent[k], axis, dim, -step))
    squares = symmetric(image_gram(full, image))
    early = sum_pair(energy, squares)
    normal = near_adjoint(image, links)
    for term in came:
        normal = normal + term.astype(f32)

    normal, rounded = lax.optimization_barrier((normal, normal.astype(bf16)))
    far = []
    for hop in HOPS:
        far.append(shifted(rounded, *hop))
    alpha = small(alpha_kernel, 1, *early)
    energy_inv = small(energy_kernel, 1, *early)
    residual = wide - combine(normal, alpha)
    fresh = lax.optimization_barrier(gram(residual, residual, lax.Precision.HIGH))
    rounded, normal_late, _ = lax.optimization_barrier((rounded, normal, energy_inv))
    near = mass_term * (normal_late - rounded.astype(f32)) + near_products(rounded, links)
    full, normal = lax.optimization_barrier((full, near))
    normal = lax.optimization_barrier(normal + hop_products((0, 1), far, links))
    normal = normal + hop_products((2, 3), far, links)
    descent = (full - combine(normal, alpha)).astype(bf16)
    late = sum_pair(fresh, gram(descent, descent))
    gamma, alpha2 = small(closing_kernel, 2, *early, energy_inv, alpha, *late)
    return combine(wide, gamma) + combine(residual, alpha2)


def solution(mesh):
    return jax.shard_map(
        body,
        mesh=mesh,
        in_specs=(
            P("groups", "ta", "xy", None, None, None),
            P("groups", None, "ta", "xy", None, None, None),
        ),
        out_specs=P("groups", "ta", "xy", None, None, None),
        check_vma=False,
    )
```
